32 devices in a mesh: layer: 8 (over z, x), col: 4 (over y, core).
Axes of the slice: x: 2, y: 2, z: 4, core: 2. Of those that a mesh axis runs over, the one named last changes fastest.
Arguments:
- l_panels: bfloat16 [8, 2048, 2048], P('layer', None, 'col'), may hold values from -6 to 6
- u_panels: bfloat16 [8, 2048, 2048], P('layer', None, 'col'), may hold values from -0.125 to 0.125
- l_masks: int32 [8, 8, 8], P('layer'), may hold values 0 or 1
- u_masks: int32 [8, 8, 8], P('layer'), may hold values 0 or 1
- ancestor_tiles: int32 [8, 8], replicated, may hold values 0 or 1
- initial: float32 [2048, 2048], P('layer', 'col'), may hold values from -6 to 6
Outputs:
- schur: float32 [2048, 2048], P('layer', 'col')
The draws below stay inside these ranges and needn't reach their ends.
All inputs are finite; a program needn't handle non-finite values. No bound on the sum of `l_masks` or of `u_masks` on one device may be relied on, other than what follows from the above.
Results may differ from the reference program's by a relative error of at most 0.0003.
Values may be sent and summed in bfloat16 or wider, within the bound.
No kernel may reach another device: no remote copies, remote signals or barrier semaphores. Data moves between devices by JAX's collectives and lax.ppermute only.
A program may use at most 64 MiB of HBM per device.

```python
import jax
import jax.numpy as jnp
from jax import lax

M = 2048
KD = 2048
TILE = 256
MT = 8
KT = 8
LAYERS = 8


def with_ends(array, stream_key, least, largest):
    longest = array.shape.index(max(array.shape))
    spots = []
    for shift in (0, 1):
        where = [jax.random.randint(jax.random.fold_in(stream_key, axis), (), 0, length) for axis, length in enumerate(array.shape)]
        where[longest] = (where[longest] + shift) % array.shape[longest]
        spots.append(tuple(where))
    return array.at[spots[0]].set(least).at[spots[1]].set(largest)


def shard_levels(rng, dims, shards, smallest, high):
    gain, own = 1.0, jax.random.fold_in(rng, 6)
    for dim, parts in shards:
        steps = jnp.exp(jax.random.uniform(jax.random.fold_in(own, dim), (parts,), jnp.float32, smallest / len(shards), high / len(shards)))
        gain = gain * jnp.repeat(steps, dims[dim] // parts).reshape([-1 if axis == dim else 1 for axis in range(len(dims))])
    return gain


def noise(own_key, shape, spread, reach, split=(), dtype=jnp.bfloat16):
    entries = spread * jax.random.normal(own_key, shape, jnp.float32)
    if split:
        entries = entries * shard_levels(own_key, shape, split, -0.22, 0.18)
    return jnp.clip(entries, -reach, reach).astype(dtype)


def setup_inputs(seed: int = 0) -> dict:
    key_of = jax.random.split(jax.random.key(seed), 7)
    return {
        "l_panels": noise(key_of[0], (LAYERS, M, KD), 1.0, 6.0, ((0, 8), (2, 4))),
        "u_panels": noise(key_of[1], (LAYERS, KD, M), KD ** -0.5, 0.125, ((0, 8), (2, 4))),
        "l_masks": with_ends((jax.random.randint(key_of[2], (LAYERS, MT, KT), 0, 2) < 1).astype(jnp.int32), jax.random.fold_in(key_of[2], 1), 0, 1),
        "u_masks": with_ends((jax.random.randint(key_of[3], (LAYERS, KT, MT), 0, 2) < 1).astype(jnp.int32), jax.random.fold_in(key_of[3], 1), 0, 1),
        "ancestor_tiles": with_ends((jax.random.randint(key_of[4], (MT, MT), 0, 4) < 3).astype(jnp.int32), jax.random.fold_in(key_of[4], 1), 0, 1),
        "initial": noise(key_of[5], (M, M), 1.0, 6.0, ((0, 8), (1, 4)), jnp.float32),
    }


def expand_tiles(mask):
    return jnp.repeat(jnp.repeat(mask, TILE, 0), TILE, 1)


def reference(l_panels, u_panels, l_masks, u_masks, ancestor_tiles, initial):
    def one_layer(total, items):
        lpanel, upanel, lmask, umask = items
        lpart = lpanel * expand_tiles(lmask).astype(jnp.bfloat16)
        upart = upanel * expand_tiles(umask).astype(jnp.bfloat16)
        return total + jnp.dot(lpart, upart, preferred_element_type=jnp.float32), None

    total, _ = lax.scan(one_layer, jnp.zeros((M, M), jnp.float32), (l_panels, u_panels, l_masks, u_masks))
    return initial - expand_tiles(ancestor_tiles).astype(jnp.float32) * total
```

```python
import functools

import jax
import jax.numpy as jnp
from jax import lax
from jax.experimental import pallas as pl
from jax.experimental.pallas import tpu as pltpu
from jax.sharding import PartitionSpec as P


def expand(mask, tile):
    return jnp.repeat(jnp.repeat(mask, tile, 0), tile, 1)


def local_plain(l_panels, u_panels, l_masks, u_masks, ancestor_tiles, initial):
    tile = l_panels.shape[1] // l_masks.shape[1]
    col_index = lax.axis_index("col")
    depth_cols = l_panels.shape[2]
    width_cols = u_panels.shape[2]
    row_count = initial.shape[0]
    lmask_mine = lax.dynamic_slice_in_dim(
        l_masks[0], col_index * (depth_cols // tile), depth_cols // tile, 1
    )
    lpanel = l_panels[0] * expand(lmask_mine, tile).astype(jnp.bfloat16)
    umask_mine = lax.dynamic_slice_in_dim(
        u_masks[0], col_index * (width_cols // tile), width_cols // tile, 1
    )
    upanel = u_panels[0] * expand(umask_mine, tile).astype(jnp.bfloat16)
    partial_total = jnp.dot(
        lax.all_gather(lpanel, "col", axis=1, tiled=True),
        upanel,
        preferred_element_type=jnp.float32,
    )
    summed = lax.psum_scatter(partial_total, "layer", scatter_dimension=0, tiled=True)
    row_ids = lax.axis_index("layer") * row_count + jnp.arange(row_count, dtype=jnp.int32)
    tile_ids = jnp.arange(ancestor_tiles.shape[0], dtype=jnp.int32)
    onehot = (row_ids[:, None] // tile == tile_ids[None, :]).astype(jnp.float32)
    row_pattern = jnp.dot(
        onehot, ancestor_tiles.astype(jnp.float32), preferred_element_type=jnp.float32
    )
    col_pattern = lax.dynamic_slice_in_dim(
        row_pattern, col_index * (width_cols // tile), width_cols // tile, 1
    )
    return initial - jnp.repeat(col_pattern, tile, 1) * summed


def block_product_body(tile, per, wide, idx, lm, um, at, l0, l1, l2, l3, u_ref, out_ref):
    row = idx[0]
    col = idx[1]
    out_ref[...] = jnp.zeros(out_ref.shape, jnp.float32)
    for j in range(wide):
        jt = col * wide + j
        for d, l_ref in enumerate((l0, l1, l2, l3)):
            for t in range(per):
                k = (col ^ d) * per + t

                @pl.when(lm[row, k] * um[k, jt] * at[row, jt] != 0)
                def _(j=j, t=t, k=k, l_ref=l_ref):
                    out_ref[:, j * tile : (j + 1) * tile] += jnp.dot(
                        l_ref[:, t * tile : (t + 1) * tile],
                        u_ref[pl.ds(pl.multiple_of(k * tile, tile), tile), j * tile : (j + 1) * tile],
                        preferred_element_type=jnp.float32,
                    )


def local_ring(l_panels, u_panels, l_masks, u_masks, ancestor_tiles, initial):
    lp, up, lm, um = l_panels[0], u_panels[0], l_masks[0], u_masks[0]
    tile = lp.shape[0] // lm.shape[0]
    per = lp.shape[1] // tile
    wide = up.shape[1] // tile
    layers = lax.axis_size("layer")
    cols = lax.axis_size("col")
    li = lax.axis_index("layer")
    ci = lax.axis_index("col")
    f32, f16 = jnp.float32, jnp.float16

    def swap(a, axis, n, d):
        return lax.ppermute(a, axis, [(i, i ^ d) for i in range(n)])

    rows = initial.shape[0]
    block = lambda r: pl.BlockSpec((rows, lp.shape[1]), lambda i, idx, *_: (idx[0], 0))
    whole = lambda a: pl.BlockSpec(a.shape, lambda i, *_: (0, 0))

    def product(rb, y, yo):
        idx = jnp.where(jnp.arange(2) == 0, rb, ci).astype(jnp.int32)
        return pl.pallas_call(
            functools.partial(block_product_body, tile, per, wide),
            grid_spec=pltpu.PrefetchScalarGridSpec(
                num_scalar_prefetch=4,
                grid=(1,),
                in_specs=[block(0), block(0), whole(y), whole(yo), whole(up)],
                out_specs=pl.BlockSpec((rows, up.shape[1]), lambda i, *_: (0, 0)),
            ),
            out_shape=jax.ShapeDtypeStruct((rows, up.shape[1]), f32),
            compiler_params=pltpu.CompilerParams(vmem_limit_bytes=16 << 20),
            name="block_product",
        )(idx, lm, um, ancestor_tiles, lp, lo, y, yo, up)

    steps = [m for m in reversed(range(layers // 2))]
    blocks = []
    for m in steps:
        blocks += [li ^ (2 * m) ^ 1, li ^ (2 * m)]
    sent = [lax.dynamic_slice_in_dim(lp, rb * rows, rows, 0) for rb in blocks]
    ys = [swap(s, "col", cols, 2) for s in sent]
    lo = swap(lp, "col", cols, 1)
    yos = [swap(y, "col", cols, 1) for y in ys]
    total = None
    for n, m in enumerate(steps):
        away = product(blocks[2 * n], ys[2 * n], yos[2 * n])
        near = product(blocks[2 * n + 1], ys[2 * n + 1], yos[2 * n + 1])
        s = near + swap(away.astype(f16), "layer", layers, 1).astype(f32)
        if m:
            s = swap(s.astype(f16), "layer", layers, 2 * m).astype(f32)
        total = s if total is None else total + s
    return initial - total


def solution(mesh):
    layers, cols = mesh.shape["layer"], mesh.shape["col"]
    return jax.shard_map(
        local_ring if (layers, cols) == (8, 4) else local_plain,
        mesh=mesh,
        in_specs=(
            P("layer", None, "col"),
            P("layer", None, "col"),
            P("layer", None, None),
            P("layer", None, None),
            P(),
            P("layer", "col"),
        ),
        out_specs=P("layer", "col"),
        check_vma=False,
    )
```

```python
import functools

import jax
import jax.numpy as jnp
from jax import lax
from jax.experimental import pallas as pl
from jax.experimental.pallas import tpu as pltpu
from jax.sharding import PartitionSpec as P


def expand(mask, tile):
    return jnp.repeat(jnp.repeat(mask, tile, 0), tile, 1)


def local_plain(l_panels, u_panels, l_masks, u_masks, ancestor_tiles, initial):
    tile = l_panels.shape[1] // l_masks.shape[1]
    col_index = lax.axis_index("col")
    depth_cols = l_panels.shape[2]
    width_cols = u_panels.shape[2]
    row_count = initial.shape[0]
    lmask_mine = lax.dynamic_slice_in_dim(
        l_masks[0], col_index * (depth_cols // tile), depth_cols // tile, 1
    )
    lpanel = l_panels[0] * expand(lmask_mine, tile).astype(jnp.bfloat16)
    umask_mine = lax.dynamic_slice_in_dim(
        u_masks[0], col_index * (width_cols // tile), width_cols // tile, 1
    )
    upanel = u_panels[0] * expand(umask_mine, tile).astype(jnp.bfloat16)
    partial_total = jnp.dot(
        lax.all_gather(lpanel, "col", axis=1, tiled=True),
        upanel,
        preferred_element_type=jnp.float32,
    )
    summed = lax.psum_scatter(partial_total, "layer", scatter_dimension=0, tiled=True)
    row_ids = lax.axis_index("layer") * row_count + jnp.arange(row_count, dtype=jnp.int32)
    tile_ids = jnp.arange(ancestor_tiles.shape[0], dtype=jnp.int32)
    onehot = (row_ids[:, None] // tile == tile_ids[None, :]).astype(jnp.float32)
    row_pattern = jnp.dot(
        onehot, ancestor_tiles.astype(jnp.float32), preferred_element_type=jnp.float32
    )
    col_pattern = lax.dynamic_slice_in_dim(
        row_pattern, col_index * (width_cols // tile), width_cols // tile, 1
    )
    return initial - jnp.repeat(col_pattern, tile, 1) * summed


def block_product_body(tile, per, wide, idx, lm, um, at, l0, l1, l2, l3, u_ref, out_ref):
    row = idx[0]
    col = idx[1]
    out_ref[...] = jnp.zeros(out_ref.shape, jnp.float32)
    for j in range(wide):
        jt = col * wide + j
        for d, l_ref in enumerate((l0, l1, l2, l3)):
            for t in range(per):
                k = (col ^ d) * per + t

                @pl.when(lm[row, k] * um[k, jt] * at[row, jt] != 0)
                def _(j=j, t=t, k=k, l_ref=l_ref):
                    out_ref[:, j * tile : (j + 1) * tile] += jnp.dot(
                        l_ref[:, t * tile : (t + 1) * tile],
                        u_ref[pl.ds(pl.multiple_of(k * tile, tile), tile), j * tile : (j + 1) * tile],
                        preferred_element_type=jnp.float32,
                    )


def local_ring(l_panels, u_panels, l_masks, u_masks, ancestor_tiles, initial):
    lp, up, lm, um = l_panels[0], u_panels[0], l_masks[0], u_masks[0]
    tile = lp.shape[0] // lm.shape[0]
    per = lp.shape[1] // tile
    wide = up.shape[1] // tile
    layers = lax.axis_size("layer")
    cols = lax.axis_size("col")
    li = lax.axis_index("layer")
    ci = lax.axis_index("col")
    f32, f16 = jnp.float32, jnp.float16

    def swap(a, axis, n, d):
        return lax.ppermute(a, axis, [(i, i ^ d) for i in range(n)])

    rows = initial.shape[0]
    block = lambda: pl.BlockSpec((rows, lp.shape[1]), lambda i, idx, *_: (idx[0], 0))
    whole = lambda a: pl.BlockSpec(a.shape, lambda i, *_: (0, 0))

    def product(rb, y, yo):
        idx = jnp.where(jnp.arange(2) == 0, rb, ci).astype(jnp.int32)
        return pl.pallas_call(
            functools.partial(block_product_body, tile, per, wide),
            grid_spec=pltpu.PrefetchScalarGridSpec(
                num_scalar_prefetch=4,
                grid=(1,),
                in_specs=[block(), block(), whole(y), whole(yo), whole(up)],
                out_specs=pl.BlockSpec((rows, up.shape[1]), lambda i, *_: (0, 0)),
            ),
            out_shape=jax.ShapeDtypeStruct((rows, up.shape[1]), f32),
            compiler_params=pltpu.CompilerParams(vmem_limit_bytes=16 << 20),
            name="block_product",
        )(idx, lm, um, ancestor_tiles, lp, lo, y, yo, up)

    steps = [m for m in reversed(range(layers // 2))]
    blocks = []
    for m in steps:
        blocks += [li ^ (2 * m) ^ 1, li ^ (2 * m)]
    sent = [lax.dynamic_slice_in_dim(lp, rb * rows, rows, 0) for rb in blocks]
    ys = [swap(s, "col", cols, 2) for s in sent]
    lo = swap(lp, "col", cols, 1)
    yos = [swap(y, "col", cols, 1) for y in ys]
    total = None
    for i, m in enumerate(steps):
        away = product(blocks[2 * i], ys[2 * i], yos[2 * i])
        near = product(blocks[2 * i + 1], ys[2 * i + 1], yos[2 * i + 1])
        s = near + swap(away.astype(f16), "layer", layers, 1).astype(f32)
        if m:
            s = swap(s.astype(f16), "layer", layers, 2 * m).astype(f32)
        total = s if total is None else total + s
    return initial - total


def solution(mesh):
    layers, cols = mesh.shape["layer"], mesh.shape["col"]
    ring = (layers, cols) == (8, 4)
    return jax.shard_map(
        local_ring if ring else local_plain,
        mesh=mesh,
        in_specs=(
            P("layer", None, "col"),
            P("layer", None, "col"),
            P("layer", None, None),
            P("layer", None, None),
            P(),
            P("layer", "col"),
        ),
        out_specs=P("layer", "col"),
        check_vma=False,
    )
```

```python
import functools

import jax
import jax.numpy as jnp
from jax import lax
from jax.experimental import pallas as pl
from jax.experimental.pallas import tpu as pltpu
from jax.sharding import PartitionSpec as P


def expand(mask, tile):
    return jnp.repeat(jnp.repeat(mask, tile, 0), tile, 1)


def local_plain(l_panels, u_panels, l_masks, u_masks, ancestor_tiles, initial):
    tile = l_panels.shape[1] // l_masks.shape[1]
    col_index = lax.axis_index("col")
    depth_cols = l_panels.shape[2]
    width_cols = u_panels.shape[2]
    row_count = initial.shape[0]
    lmask_mine = lax.dynamic_slice_in_dim(
        l_masks[0], col_index * (depth_cols // tile), depth_cols // tile, 1
    )
    lpanel = l_panels[0] * expand(lmask_mine, tile).astype(jnp.bfloat16)
    umask_mine = lax.dynamic_slice_in_dim(
        u_masks[0], col_index * (width_cols // tile), width_cols // tile, 1
    )
    upanel = u_panels[0] * expand(umask_mine, tile).astype(jnp.bfloat16)
    partial_total = jnp.dot(
        lax.all_gather(lpanel, "col", axis=1, tiled=True),
        upanel,
        preferred_element_type=jnp.float32,
    )
    summed = lax.psum_scatter(partial_total, "layer", scatter_dimension=0, tiled=True)
    row_ids = lax.axis_index("layer") * row_count + jnp.arange(row_count, dtype=jnp.int32)
    tile_ids = jnp.arange(ancestor_tiles.shape[0], dtype=jnp.int32)
    onehot = (row_ids[:, None] // tile == tile_ids[None, :]).astype(jnp.float32)
    row_pattern = jnp.dot(
        onehot, ancestor_tiles.astype(jnp.float32), preferred_element_type=jnp.float32
    )
    col_pattern = lax.dynamic_slice_in_dim(
        row_pattern, col_index * (width_cols // tile), width_cols // tile, 1
    )
    return initial - jnp.repeat(col_pattern, tile, 1) * summed


CAPS = (2, 4, 7, 10, 12)
GROUPS = ((0,), (1,), (2, 3), (4, 5), (6, 7))


def row_block(n, layers, li):
    return li ^ (2 * (layers // 2 - 1 - n // 2)) ^ (1 - n % 2)


def scan(lm, um, at, li, owner, dest, layers, per, wide):
    first = (dest // 2) * 2 * wide
    ubits = [sum(um[owner * per + t, first + j] << j for j in range(2 * wide)) for t in range(per)]
    needs = []
    for n in range(layers):
        rb = row_block(n, layers, li)
        abits = sum(at[rb, first + j] << j for j in range(2 * wide))
        for t in range(per):
            hit = jnp.logical_and(lm[rb, owner * per + t] != 0, (abits & ubits[t]) != 0)
            needs.append((n, t, rb, hit.astype(jnp.int32)))
    return needs


def late_ranges(per):
    spots, base = [], 0
    for g, group in enumerate(GROUPS):
        missing = (group[-1] + 1) * per - CAPS[g]
        if missing > 0:
            spots.append((g, base, CAPS[g], CAPS[g] + missing))
            base += missing
    return spots, base


def pack_copies(needs, lp, places, tile, sems):
    copies, rank = [], jnp.int32(0)
    for e, (n, t, rb, hit) in enumerate(needs):
        for q, (batch, base, lo, hi) in enumerate(places):
            if e < lo:
                continue
            go = jnp.logical_and(hit != 0, jnp.logical_and(rank >= lo, rank < hi))
            slot = base + jnp.clip(rank - lo, 0, hi - lo - 1)
            copy = pltpu.make_async_copy(
                lp.at[pl.ds(pl.multiple_of(rb * tile, tile), tile), t * tile : (t + 1) * tile],
                batch.at[pl.ds(pl.multiple_of(slot * tile, tile), tile), :],
                sems.at[q, e],
            )
            copies.append((go, copy))
        rank = rank + hit
    for go, copy in copies:
        pl.when(go)(copy.start)
    return copies


def first_batch_body(dims, lm_hbm, um_hbm, at_hbm, lp, b0, lm, um, at, sems):
    layers, _, per, wide, tile = dims
    loads = [
        pltpu.make_async_copy(src, dst, sems.at[1, i])
        for i, (src, dst) in enumerate(((lm_hbm, lm), (um_hbm, um), (at_hbm, at)))
    ]
    for load in loads:
        load.start()
    for load in loads:
        load.wait()
    li, ci = lax.axis_index("layer"), lax.axis_index("col")
    needs = scan(lm, um, at, li, ci, ci ^ 2, layers, per, wide)
    for go, copy in pack_copies(needs, lp, [(b0, 0, 0, CAPS[0])], tile, sems):
        pl.when(go)(copy.wait)


def other_batches_body(dims, lm, um, at, lp, *refs):
    layers, cols, per, wide, tile = dims
    *batches, late, ranks, flag, sems = refs
    li, ci = lax.axis_index("layer"), lax.axis_index("col")
    mine = scan(lm, um, at, li, ci, ci ^ 2, layers, per, wide)
    places = [(b, 0, lo, hi) for b, lo, hi in zip(batches, CAPS[:-1], CAPS[1:])]
    places += [(late, base, lo, hi) for _, base, lo, hi in late_ranges(per)[0]]
    copies = pack_copies(mine, lp, places, tile, sems)
    counts = []
    for o in range(cols):
        needs = mine if o == 0 else scan(lm, um, at, li, ci ^ o, ci ^ o ^ 2, layers, per, wide)
        rank, at_end = jnp.int32(0), {}
        for e, (n, t, _, hit) in enumerate(needs):
            if o >= 2:
                ranks[(o - 2) * layers * per + e] = rank
            rank = rank + hit
            at_end[n] = rank
        counts.append(at_end)
    short = jnp.bool_(False)
    for g, group in enumerate(GROUPS):
        for c in counts:
            short = jnp.logical_or(short, c[group[-1]] > CAPS[g])
    flag[0] = short.astype(jnp.int32)
    for go, copy in copies:
        pl.when(go)(copy.wait)


def product_body(dims, g, lm, um, at, ranks, lp, lo, up, *refs):
    layers, cols, per, wide, tile = dims
    group = GROUPS[g]
    count = g + 2
    spare = [r for r in late_ranges(per)[0] if r[0] == g]
    direct, relayed = refs[:count], refs[count : 2 * count]
    outs = refs[2 * count : 2 * count + len(group)]
    u_vmem, tiles, u_sem, sems = refs[2 * count + len(group) :]
    li, ci = lax.axis_index("layer"), lax.axis_index("col")
    u_copy = pltpu.make_async_copy(up, u_vmem, u_sem)
    u_copy.start()
    ranges = [(q, 0, lo, hi) for q, (lo, hi) in enumerate(zip((0, *CAPS[:g]), CAPS[: g + 1]))]
    ranges += [(g + 1, base, lo, hi) for _, base, lo, hi in spare]
    work = []
    for a, n in enumerate(group):
        rb = row_block(n, layers, li)
        keep = [at[rb, ci * wide + j] for j in range(wide)]
        for d in range(cols):
            for t in range(per):
                k = (ci ^ d) * per + t
                on = lm[rb, k]
                uses = [on * um[k, ci * wide + j] * keep[j] != 0 for j in range(wide)]
                use = functools.reduce(jnp.logical_or, uses)
                slot = len(work)
                target, sem = tiles.at[slot], sems.at[slot]

                def begin(go, source, target=target, sem=sem):
                    copy = pltpu.make_async_copy(source, target, sem)
                    pl.when(go)(copy.start)
                    return copy

                if d < 2:
                    source = (lp, lo)[d].at[
                        pl.ds(pl.multiple_of(rb * tile, tile), tile), t * tile : (t + 1) * tile
                    ]
                    copy = begin(use, source)
                else:
                    rank = ranks[(d - 2) * layers * per + n * per + t]
                    for q, base, first, end in ranges:
                        if first > n * per + t:
                            continue
                        batch = (direct, relayed)[d - 2][q]
                        spot = base + jnp.clip(rank - first, 0, end - first - 1)
                        go = jnp.logical_and(use, jnp.logical_and(rank >= first, rank < end))
                        copy = begin(go, batch.at[pl.ds(pl.multiple_of(spot * tile, tile), tile), :])
                work.append((a, k, use, uses, copy))
    for out in outs:
        out[...] = jnp.zeros(out.shape, jnp.float32)
    u_copy.wait()
    for slot, (a, k, use, uses, copy) in enumerate(work):

        @pl.when(use)
        def _(slot=slot, a=a, k=k, uses=uses, copy=copy):
            copy.wait()
            for j in range(wide):

                @pl.when(uses[j])
                def _(j=j):
                    outs[a][:, j * tile : (j + 1) * tile] += jnp.dot(
                        tiles[slot],
                        u_vmem[pl.ds(pl.multiple_of(k * tile, tile), tile), j * tile : (j + 1) * tile],
                        preferred_element_type=jnp.float32,
                    )


def local_ring(l_panels, u_panels, l_masks, u_masks, ancestor_tiles, initial):
    lp, up, lm, um = l_panels[0], u_panels[0], l_masks[0], u_masks[0]
    tile = lp.shape[0] // lm.shape[0]
    per = lp.shape[1] // tile
    wide = up.shape[1] // tile
    layers = lax.axis_size("layer")
    cols = lax.axis_size("col")
    dims = (layers, cols, per, wide, tile)
    f32, f16 = jnp.float32, jnp.float16
    rows = initial.shape[0]
    spare = late_ranges(per)[1]
    smem = pl.BlockSpec(memory_space=pltpu.SMEM)
    anywhere = pl.BlockSpec(memory_space=pl.ANY)
    vmem = pl.BlockSpec(memory_space=pltpu.VMEM)
    panel = lambda n: jax.ShapeDtypeStruct((n * tile, tile), lp.dtype)
    tables = (lm, um, ancestor_tiles)
    in_hbm = lambda a: pltpu.with_memory_space_constraint(a, pltpu.HBM)
    in_vmem = lambda a: pltpu.with_memory_space_constraint(a, pltpu.VMEM)
    params = pltpu.CompilerParams(vmem_limit_bytes=8 << 20)

    def swap(a, axis, n, d):
        return lax.ppermute(a, axis, [(i, i ^ d) for i in range(n)])

    def first_batch():
        return pl.pallas_call(
            functools.partial(first_batch_body, dims),
            in_specs=[anywhere] * 4,
            out_specs=anywhere,
            out_shape=panel(CAPS[0]),
            scratch_shapes=[pltpu.SMEM(a.shape, a.dtype) for a in tables]
            + [pltpu.SemaphoreType.DMA((2, layers * per))],
            compiler_params=params,
            name="first_batch",
        )(*map(in_hbm, tables), in_hbm(lp))

    def other_batches():
        sizes = [b - a for a, b in zip(CAPS[:-1], CAPS[1:])] + [spare]
        *batches, late, ranks, flag = pl.pallas_call(
            functools.partial(other_batches_body, dims),
            in_specs=[smem] * 3 + [anywhere],
            out_specs=[anywhere] * len(sizes) + [smem, smem],
            out_shape=[panel(n) for n in sizes]
            + [jax.ShapeDtypeStruct((2 * layers * per,), jnp.int32), jax.ShapeDtypeStruct((1,), jnp.int32)],
            scratch_shapes=[pltpu.SemaphoreType.DMA((len(sizes) + len(GROUPS), layers * per))],
            compiler_params=params,
            name="other_batches",
        )(*tables, in_vmem(lp))
        return batches, late, ranks, flag[0]

    def product(g, direct, relayed):
        group = GROUPS[g]
        return pl.pallas_call(
            functools.partial(product_body, dims, g),
            in_specs=[smem] * 4 + [anywhere] * (3 + len(direct) + len(relayed)),
            out_specs=[vmem] * len(group),
            out_shape=[jax.ShapeDtypeStruct((rows, up.shape[1]), f32)] * len(group),
            scratch_shapes=[
                pltpu.VMEM(up.shape, up.dtype),
                pltpu.VMEM((len(group) * cols * per, tile, tile), lp.dtype),
                pltpu.SemaphoreType.DMA,
                pltpu.SemaphoreType.DMA((len(group) * cols * per,)),
            ],
            compiler_params=params,
            name="product",
        )(*tables, ranks, in_vmem(lp), in_vmem(lo), in_vmem(up), *direct, *relayed)

    b0 = first_batch()
    batches, late, ranks, flag = other_batches()
    batches = [b0, *batches]
    ys = [swap(b, "col", cols, 2) for b in batches]
    lo = swap(lp, "col", cols, 1)

    def fetch(b):
        y = swap(b, "col", cols, 2)
        return y, swap(y, "col", cols, 1)

    def unused(b):
        return pl.pallas_call(
            lambda *refs: None,
            out_specs=[anywhere] * 2,
            out_shape=[panel(spare)] * 2,
            compiler_params=params,
            name="unused",
        )()

    late, late_o = lax.cond(flag != 0, fetch, unused, late)
    yos = [swap(y, "col", cols, 1) for y in ys]
    parts = []
    for g in range(len(GROUPS)):
        parts += product(g, [*ys[: g + 1], late], [*yos[: g + 1], late_o])
    total = None
    for i in range(layers // 2):
        m = layers // 2 - 1 - i
        away, near = parts[2 * i], parts[2 * i + 1]
        far = swap(away.astype(f16), "layer", layers, 1)
        s = near + far.astype(f32)
        if m:
            s = s.astype(f16)
        if m:
            s = swap(s, "layer", layers, 2 * m).astype(f32)
        total = s if total is None else total + s
    return initial - total


def solution(mesh):
    layers, cols = mesh.shape["layer"], mesh.shape["col"]
    ring = (layers, cols) == (8, 4)
    return jax.shard_map(
        local_ring if ring else local_plain,
        mesh=mesh,
        in_specs=(
            P("layer", None, "col"),
            P("layer", None, "col"),
            P("layer", None, None),
            P("layer", None, None),
            P(),
            P("layer", "col"),
        ),
        out_specs=P("layer", "col"),
        check_vma=False,
    )
```

```python
import functools

import jax
import jax.numpy as jnp
from jax import lax
from jax.experimental import pallas as pl
from jax.experimental.pallas import tpu as pltpu
from jax.sharding import PartitionSpec as P


def expand(mask, tile):
    return jnp.repeat(jnp.repeat(mask, tile, 0), tile, 1)


def local_plain(l_panels, u_panels, l_masks, u_masks, ancestor_tiles, initial):
    tile = l_panels.shape[1] // l_masks.shape[1]
    col_index = lax.axis_index("col")
    depth_cols = l_panels.shape[2]
    width_cols = u_panels.shape[2]
    row_count = initial.shape[0]
    lmask_mine = lax.dynamic_slice_in_dim(
        l_masks[0], col_index * (depth_cols // tile), depth_cols // tile, 1
    )
    lpanel = l_panels[0] * expand(lmask_mine, tile).astype(jnp.bfloat16)
    umask_mine = lax.dynamic_slice_in_dim(
        u_masks[0], col_index * (width_cols // tile), width_cols // tile, 1
    )
    upanel = u_panels[0] * expand(umask_mine, tile).astype(jnp.bfloat16)
    partial_total = jnp.dot(
        lax.all_gather(lpanel, "col", axis=1, tiled=True),
        upanel,
        preferred_element_type=jnp.float32,
    )
    summed = lax.psum_scatter(partial_total, "layer", scatter_dimension=0, tiled=True)
    row_ids = lax.axis_index("layer") * row_count + jnp.arange(row_count, dtype=jnp.int32)
    tile_ids = jnp.arange(ancestor_tiles.shape[0], dtype=jnp.int32)
    onehot = (row_ids[:, None] // tile == tile_ids[None, :]).astype(jnp.float32)
    row_pattern = jnp.dot(
        onehot, ancestor_tiles.astype(jnp.float32), preferred_element_type=jnp.float32
    )
    col_pattern = lax.dynamic_slice_in_dim(
        row_pattern, col_index * (width_cols // tile), width_cols // tile, 1
    )
    return initial - jnp.repeat(col_pattern, tile, 1) * summed


BLOCKS = ((3, 1), (3, 0), (2, 1), (2, 0), (1, 1), (0, 1), (1, 0), (0, 0))


def row_block(n, li):
    distance, away = BLOCKS[n]
    return li ^ (2 * distance) ^ away


def take_body(blocks, lp, *refs):
    *outs, sems = refs
    li = lax.axis_index("layer")
    copies = []
    for i, (n, out) in enumerate(zip(blocks, outs)):
        rows = out.shape[0]
        start = pl.multiple_of(row_block(n, li) * rows, rows)
        copies.append(pltpu.make_async_copy(lp.at[pl.ds(start, rows), :], out, sems.at[i]))
    for copy in copies:
        copy.start()
    for copy in copies:
        copy.wait()


def product_body(dims, n, lm, um, at, l0, l1, l2, l3, u_ref, out):
    _, _, per, wide, tile = dims
    li, ci = lax.axis_index("layer"), lax.axis_index("col")
    rb = row_block(n, li)
    rows = out.shape[0]
    out[...] = jnp.zeros(out.shape, jnp.float32)
    for d, ref in enumerate((l0, l1, l2, l3)):
        for t in range(per):
            k = (ci ^ d) * per + t
            on = lm[rb, k]
            for j in range(wide):
                jt = ci * wide + j

                @pl.when(on * um[k, jt] * at[rb, jt] != 0)
                def _(d=d, ref=ref, t=t, k=k, j=j):
                    start = pl.multiple_of(rb * rows, rows) if d == 1 else 0
                    out[:, j * tile : (j + 1) * tile] += jnp.dot(
                        ref[pl.ds(start, rows), t * tile : (t + 1) * tile],
                        u_ref[pl.ds(pl.multiple_of(k * tile, tile), tile), j * tile : (j + 1) * tile],
                        preferred_element_type=jnp.float32,
                    )


def local_ring(l_panels, u_panels, l_masks, u_masks, ancestor_tiles, initial):
    lp, up, lm, um = l_panels[0], u_panels[0], l_masks[0], u_masks[0]
    tile = lp.shape[0] // lm.shape[0]
    per = lp.shape[1] // tile
    wide = up.shape[1] // tile
    layers = lax.axis_size("layer")
    cols = lax.axis_size("col")
    dims = (layers, cols, per, wide, tile)
    f32, f16 = jnp.float32, jnp.float16
    rows = initial.shape[0]
    smem = pl.BlockSpec(memory_space=pltpu.SMEM)
    vmem = pl.BlockSpec(memory_space=pltpu.VMEM)
    hbm = pl.BlockSpec(memory_space=pltpu.HBM)
    in_hbm = lambda a: pltpu.with_memory_space_constraint(a, pltpu.HBM)
    in_vmem = lambda a: pltpu.with_memory_space_constraint(a, pltpu.VMEM)
    params = pltpu.CompilerParams(vmem_limit_bytes=8 << 20)

    def swap(a, axis, n, d):
        return lax.ppermute(a, axis, [(i, i ^ d) for i in range(n)])

    def take(blocks):
        return pl.pallas_call(
            functools.partial(take_body, blocks),
            in_specs=[hbm],
            out_specs=[vmem] * len(blocks),
            out_shape=[jax.ShapeDtypeStruct((rows, lp.shape[1]), lp.dtype)] * len(blocks),
            scratch_shapes=[pltpu.SemaphoreType.DMA((len(blocks),))],
            compiler_params=params,
            name="take",
        )(in_hbm(lp))

    def product(n, mine, other, y, yo):
        return pl.pallas_call(
            functools.partial(product_body, dims, n),
            in_specs=[smem] * 3 + [vmem] * 5,
            out_specs=vmem,
            out_shape=jax.ShapeDtypeStruct((rows, up.shape[1]), f32),
            compiler_params=params,
            name="product",
        )(lm, um, ancestor_tiles, mine, in_vmem(other), y, yo, in_vmem(up))

    sent = take((0,)) + take(tuple(range(1, layers)))
    ys = [swap(s, "col", cols, 2) for s in sent]
    lo = swap(lp, "col", cols, 1)
    yos = [swap(y, "col", cols, 1) for y in ys]
    parts = [product(n, sent[n], lo, ys[n], yos[n]) for n in range(layers)]
    for p in range(layers // 2):
        far = swap(parts[BLOCKS.index((3 - p, 1))].astype(f16), "layer", layers, 1)
        s = parts[BLOCKS.index((3 - p, 0))] + far.astype(f32)
        if p == 1:
            s = s + beside.astype(f32)
        if p == 3:
            s = initial - s
        else:
            s = s.astype(f16)
        if p == 0:
            beside = swap(s, "layer", layers, 2)
        if p == 1:
            across = swap(s, "layer", layers, 4)
        if p == 2:
            last = swap(s, "layer", layers, 2)
    return s - across.astype(f32) - last.astype(f32)


def solution(mesh):
    layers, cols = mesh.shape["layer"], mesh.shape["col"]
    ring = (layers, cols) == (8, 4)
    return jax.shard_map(
        local_ring if ring else local_plain,
        mesh=mesh,
        in_specs=(
            P("layer", None, "col"),
            P("layer", None, "col"),
            P("layer", None, None),
            P("layer", None, None),
            P(),
            P("layer", "col"),
        ),
        out_specs=P("layer", "col"),
        check_vma=False,
    )
```

```python
import functools

import jax
import jax.numpy as jnp
from jax import lax
from jax.experimental import pallas as pl
from jax.experimental.pallas import tpu as pltpu
from jax.sharding import PartitionSpec as P


def expand(mask, tile):
    return jnp.repeat(jnp.repeat(mask, tile, 0), tile, 1)


def local_plain(l_panels, u_panels, l_masks, u_masks, ancestor_tiles, initial):
    tile = l_panels.shape[1] // l_masks.shape[1]
    col_index = lax.axis_index("col")
    depth_cols = l_panels.shape[2]
    width_cols = u_panels.shape[2]
    row_count = initial.shape[0]
    lmask_mine = lax.dynamic_slice_in_dim(
        l_masks[0], col_index * (depth_cols // tile), depth_cols // tile, 1
    )
    lpanel = l_panels[0] * expand(lmask_mine, tile).astype(jnp.bfloat16)
    umask_mine = lax.dynamic_slice_in_dim(
        u_masks[0], col_index * (width_cols // tile), width_cols // tile, 1
    )
    upanel = u_panels[0] * expand(umask_mine, tile).astype(jnp.bfloat16)
    partial_total = jnp.dot(
        lax.all_gather(lpanel, "col", axis=1, tiled=True),
        upanel,
        preferred_element_type=jnp.float32,
    )
    summed = lax.psum_scatter(partial_total, "layer", scatter_dimension=0, tiled=True)
    row_ids = lax.axis_index("layer") * row_count + jnp.arange(row_count, dtype=jnp.int32)
    tile_ids = jnp.arange(ancestor_tiles.shape[0], dtype=jnp.int32)
    onehot = (row_ids[:, None] // tile == tile_ids[None, :]).astype(jnp.float32)
    row_pattern = jnp.dot(
        onehot, ancestor_tiles.astype(jnp.float32), preferred_element_type=jnp.float32
    )
    col_pattern = lax.dynamic_slice_in_dim(
        row_pattern, col_index * (width_cols // tile), width_cols // tile, 1
    )
    return initial - jnp.repeat(col_pattern, tile, 1) * summed


CHUNKS = (
    (3, 1, 0, 1),
    (2, 1, 0, 1),
    (3, 0, 0, 1),
    (2, 0, 0, 1),
    (1, 1, 0, 1),
    (0, 1, 0, 1),
    (1, 0, 0, 1),
    (0, 0, 0, 1),
)


def row_block(n, li):
    distance, away, _, _ = CHUNKS[n]
    return li ^ (2 * distance) ^ away


def row_start(n, li, rows):
    _, _, part, parts = CHUNKS[n]
    return pl.multiple_of((row_block(n, li) * parts + part) * rows, rows)


def take_body(chunks, lp, *refs):
    *outs, sems = refs
    li = lax.axis_index("layer")
    copies = []
    for i, (n, out) in enumerate(zip(chunks, outs)):
        rows = out.shape[0]
        start = row_start(n, li, rows)
        copies.append(pltpu.make_async_copy(lp.at[pl.ds(start, rows), :], out, sems.at[i]))
    for copy in copies:
        copy.start()
    for copy in copies:
        copy.wait()


def product_body(dims, n, ds, lm, um, at, *refs):
    _, _, per, wide, tile = dims
    *panels, u_ref, out = refs
    li, ci = lax.axis_index("layer"), lax.axis_index("col")
    rb = row_block(n, li)
    rows = out.shape[0]
    if len(panels) > len(ds):
        panels = panels[1:]
    else:
        out[...] = jnp.zeros(out.shape, jnp.float32)
    for d, ref in zip(ds, panels):
        for t in range(per):
            k = (ci ^ d) * per + t
            on = lm[rb, k]
            for j in range(wide):
                jt = ci * wide + j

                @pl.when(on * um[k, jt] * at[rb, jt] != 0)
                def _(d=d, ref=ref, t=t, k=k, j=j):
                    start = row_start(n, li, rows) if d == 1 else 0
                    out[:, j * tile : (j + 1) * tile] += jnp.dot(
                        ref[pl.ds(start, rows), t * tile : (t + 1) * tile],
                        u_ref[pl.ds(pl.multiple_of(k * tile, tile), tile), j * tile : (j + 1) * tile],
                        preferred_element_type=jnp.float32,
                    )


def local_ring(l_panels, u_panels, l_masks, u_masks, ancestor_tiles, initial):
    lp, up, lm, um = l_panels[0], u_panels[0], l_masks[0], u_masks[0]
    tile = lp.shape[0] // lm.shape[0]
    per = lp.shape[1] // tile
    wide = up.shape[1] // tile
    layers = lax.axis_size("layer")
    cols = lax.axis_size("col")
    dims = (layers, cols, per, wide, tile)
    f32, f16 = jnp.float32, jnp.float16
    rows = initial.shape[0]
    smem = pl.BlockSpec(memory_space=pltpu.SMEM)
    vmem = pl.BlockSpec(memory_space=pltpu.VMEM)
    hbm = pl.BlockSpec(memory_space=pltpu.HBM)
    in_hbm = lambda a: pltpu.with_memory_space_constraint(a, pltpu.HBM)
    in_vmem = lambda a: pltpu.with_memory_space_constraint(a, pltpu.VMEM)
    params = pltpu.CompilerParams(vmem_limit_bytes=8 << 20)

    def swap(a, axis, n, d):
        return lax.ppermute(a, axis, [(i, i ^ d) for i in range(n)])

    count = lambda n: rows // CHUNKS[n][3]

    def take(chunks):
        return pl.pallas_call(
            functools.partial(take_body, chunks),
            in_specs=[hbm],
            out_specs=[vmem] * len(chunks),
            out_shape=[jax.ShapeDtypeStruct((count(n), lp.shape[1]), lp.dtype) for n in chunks],
            scratch_shapes=[pltpu.SemaphoreType.DMA((len(chunks),))],
            compiler_params=params,
            name="take",
        )(in_hbm(lp))

    def product(n, ds, panels, so_far=()):
        return pl.pallas_call(
            functools.partial(product_body, dims, n, ds),
            in_specs=[smem] * 3 + [vmem] * (len(so_far) + len(ds) + 1),
            out_specs=vmem,
            out_shape=jax.ShapeDtypeStruct((count(n), up.shape[1]), f32),
            input_output_aliases={3: 0} if so_far else {},
            compiler_params=params,
            name="product",
        )(lm, um, ancestor_tiles, *so_far, *panels, in_vmem(up))

    sent = take((0,)) + take(tuple(range(1, len(CHUNKS))))
    ys = [swap(s, "col", cols, 2) for s in sent]
    lo = swap(lp, "col", cols, 1)
    yos = [swap(y, "col", cols, 1) for y in ys]
    lo = in_vmem(lo)
    early = [product(n, (0, 1), (sent[n], lo)) for n in range(len(CHUNKS))]
    parts = []
    for n, so_far in enumerate(early):
        if n in WAITING:
            so_far = product(n, (2,), (ys[n],), (so_far,))
            parts.append(product(n, (3,), (yos[n],), (so_far,)))
        else:
            parts.append(product(n, (2, 3), (ys[n], yos[n]), (so_far,)))

    def pieces(distance, away):
        return [n for n, c in enumerate(CHUNKS) if c[:2] == (distance, away)]

    def join(a):
        return a[0] if len(a) == 1 else jnp.concatenate(a)

    def over_x(distance):
        found = pieces(distance, 1)
        return join([swap(parts[n].astype(f16), "layer", layers, 1) for n in found])

    def summed(distance, far, more=None):
        found, out = pieces(distance, 0), []
        for i, n in enumerate(found):
            at = slice(i * count(n), (i + 1) * count(n))
            mine = parts[n]
            if out:
                mine, _ = lax.optimization_barrier((mine, out[-1]))
            s = mine + far[at].astype(f32)
            if more is not None:
                s = s + more[at].astype(f32)
            out.append(s if distance == 0 else s.astype(f16))
        return out

    def over_z(sums, d):
        return join([swap(s, "layer", layers, d) for s in sums])

    beside = over_z(summed(3, over_x(3)), 2)
    across = over_z(summed(2, over_x(2), beside), 4)
    last = over_z(summed(1, over_x(1)), 2)
    own = join(summed(0, over_x(0)))
    rest = lax.optimization_barrier(initial - own - across.astype(f32))
    return rest - last.astype(f32)


WAITING = (6, 7)


def solution(mesh):
    layers, cols = mesh.shape["layer"], mesh.shape["col"]
    ring = (layers, cols) == (8, 4)
    return jax.shard_map(
        local_ring if ring else local_plain,
        mesh=mesh,
        in_specs=(
            P("layer", None, "col"),
            P("layer", None, "col"),
            P("layer", None, None),
            P("layer", None, None),
            P(),
            P("layer", "col"),
        ),
        out_specs=P("layer", "col"),
        check_vma=False,
    )
```

```python
import functools

import jax
import jax.numpy as jnp
from jax import lax
from jax.experimental import pallas as pl
from jax.experimental.pallas import tpu as pltpu
from jax.sharding import PartitionSpec as P


def expand(mask, tile):
    return jnp.repeat(jnp.repeat(mask, tile, 0), tile, 1)


def local_plain(l_panels, u_panels, l_masks, u_masks, ancestor_tiles, initial):
    tile = l_panels.shape[1] // l_masks.shape[1]
    col_index = lax.axis_index("col")
    depth_cols = l_panels.shape[2]
    width_cols = u_panels.shape[2]
    row_count = initial.shape[0]
    lmask_mine = lax.dynamic_slice_in_dim(
        l_masks[0], col_index * (depth_cols // tile), depth_cols // tile, 1
    )
    lpanel = l_panels[0] * expand(lmask_mine, tile).astype(jnp.bfloat16)
    umask_mine = lax.dynamic_slice_in_dim(
        u_masks[0], col_index * (width_cols // tile), width_cols // tile, 1
    )
    upanel = u_panels[0] * expand(umask_mine, tile).astype(jnp.bfloat16)
    partial_total = jnp.dot(
        lax.all_gather(lpanel, "col", axis=1, tiled=True),
        upanel,
        preferred_element_type=jnp.float32,
    )
    summed = lax.psum_scatter(partial_total, "layer", scatter_dimension=0, tiled=True)
    row_ids = lax.axis_index("layer") * row_count + jnp.arange(row_count, dtype=jnp.int32)
    tile_ids = jnp.arange(ancestor_tiles.shape[0], dtype=jnp.int32)
    onehot = (row_ids[:, None] // tile == tile_ids[None, :]).astype(jnp.float32)
    row_pattern = jnp.dot(
        onehot, ancestor_tiles.astype(jnp.float32), preferred_element_type=jnp.float32
    )
    col_pattern = lax.dynamic_slice_in_dim(
        row_pattern, col_index * (width_cols // tile), width_cols // tile, 1
    )
    return initial - jnp.repeat(col_pattern, tile, 1) * summed


CHUNKS = (
    (3, 1, 0, 1),
    (3, 0, 0, 1),
    (2, 1, 0, 1),
    (2, 0, 0, 1),
    (1, 1, 0, 1),
    (0, 1, 0, 1),
    (1, 0, 0, 1),
    (0, 0, 0, 1),
)


def row_block(n, li):
    distance, away, _, _ = CHUNKS[n]
    return li ^ (2 * distance) ^ away


def row_start(n, li, rows):
    _, _, part, parts = CHUNKS[n]
    return pl.multiple_of((row_block(n, li) * parts + part) * rows, rows)


def take_body(chunks, lp, *refs):
    *outs, sems = refs
    li = lax.axis_index("layer")
    copies = []
    for i, (n, out) in enumerate(zip(chunks, outs)):
        rows = out.shape[0]
        start = row_start(n, li, rows)
        copies.append(pltpu.make_async_copy(lp.at[pl.ds(start, rows), :], out, sems.at[i]))
    for copy in copies:
        copy.start()
    for copy in copies:
        copy.wait()


def product_body(dims, n, ds, lm, um, at, *refs):
    _, _, per, wide, tile = dims
    *panels, u_ref, out = refs
    li, ci = lax.axis_index("layer"), lax.axis_index("col")
    rb = row_block(n, li)
    rows = out.shape[0]
    if len(panels) > len(ds):
        panels = panels[1:]
    else:
        out[...] = jnp.zeros(out.shape, jnp.float32)
    for d, ref in zip(ds, panels):
        for t in range(per):
            k = (ci ^ d) * per + t
            on = lm[rb, k]
            for j in range(wide):
                jt = ci * wide + j

                @pl.when(on * um[k, jt] * at[rb, jt] != 0)
                def _(d=d, ref=ref, t=t, k=k, j=j):
                    start = row_start(n, li, rows) if d == 1 else 0
                    out[:, j * tile : (j + 1) * tile] += jnp.dot(
                        ref[pl.ds(start, rows), t * tile : (t + 1) * tile],
                        u_ref[pl.ds(pl.multiple_of(k * tile, tile), tile), j * tile : (j + 1) * tile],
                        preferred_element_type=jnp.float32,
                    )


def local_ring(l_panels, u_panels, l_masks, u_masks, ancestor_tiles, initial):
    lp, up, lm, um = l_panels[0], u_panels[0], l_masks[0], u_masks[0]
    tile = lp.shape[0] // lm.shape[0]
    per = lp.shape[1] // tile
    wide = up.shape[1] // tile
    layers = lax.axis_size("layer")
    cols = lax.axis_size("col")
    dims = (layers, cols, per, wide, tile)
    f32, f16 = jnp.float32, jnp.float16
    rows = initial.shape[0]
    smem = pl.BlockSpec(memory_space=pltpu.SMEM)
    vmem = pl.BlockSpec(memory_space=pltpu.VMEM)
    hbm = pl.BlockSpec(memory_space=pltpu.HBM)
    in_hbm = lambda a: pltpu.with_memory_space_constraint(a, pltpu.HBM)
    in_vmem = lambda a: pltpu.with_memory_space_constraint(a, pltpu.VMEM)
    params = pltpu.CompilerParams(vmem_limit_bytes=8 << 20)

    def swap(a, axis, n, d):
        return lax.ppermute(a, axis, [(i, i ^ d) for i in range(n)])

    count = lambda n: rows // CHUNKS[n][3]

    def take(chunks):
        return pl.pallas_call(
            functools.partial(take_body, chunks),
            in_specs=[hbm],
            out_specs=[vmem] * len(chunks),
            out_shape=[jax.ShapeDtypeStruct((count(n), lp.shape[1]), lp.dtype) for n in chunks],
            scratch_shapes=[pltpu.SemaphoreType.DMA((len(chunks),))],
            compiler_params=params,
            name="take",
        )(in_hbm(lp))

    def product(n, ds, panels, so_far=()):
        return pl.pallas_call(
            functools.partial(product_body, dims, n, ds),
            in_specs=[smem] * 3 + [vmem] * (len(so_far) + len(ds) + 1),
            out_specs=vmem,
            out_shape=jax.ShapeDtypeStruct((count(n), up.shape[1]), f32),
            input_output_aliases={3: 0} if so_far else {},
            compiler_params=params,
            name="product",
        )(lm, um, ancestor_tiles, *so_far, *panels, in_vmem(up))

    sent = take((0,)) + take(tuple(range(1, len(CHUNKS))))
    ys = [swap(s, "col", cols, 2) for s in sent]
    lo = swap(lp, "col", cols, 1)
    yos = [swap(y, "col", cols, 1) for y in ys]
    lo = in_vmem(lo)
    early = [product(n, (0, 1), (sent[n], lo)) for n in range(len(CHUNKS))]
    parts = [product(n, (2, 3), (ys[n], yos[n]), (early[n],)) for n in range(len(CHUNKS))]

    def pieces(distance, away):
        return [n for n, c in enumerate(CHUNKS) if c[:2] == (distance, away)]

    def join(a):
        return a[0] if len(a) == 1 else jnp.concatenate(a)

    def over_x(distance):
        found = pieces(distance, 1)
        return join([swap(parts[n].astype(f16), "layer", layers, 1) for n in found])

    def summed(distance, far, more=None):
        found, out = pieces(distance, 0), []
        for i, n in enumerate(found):
            at = slice(i * count(n), (i + 1) * count(n))
            mine = parts[n]
            if out:
                mine, _ = lax.optimization_barrier((mine, out[-1]))
            s = mine + far[at].astype(f32)
            if more is not None:
                s = s + more[at].astype(f32)
            out.append(s if distance == 0 else s.astype(f16))
        return out

    def over_z(sums, d):
        return join([swap(s, "layer", layers, d) for s in sums])

    beside = over_z(summed(3, over_x(3)), 2)
    across = over_z(summed(2, over_x(2), beside), 4)
    last = over_z(summed(1, over_x(1)), 2)
    own = join(summed(0, over_x(0)))
    rest = lax.optimization_barrier(initial - own - across.astype(f32))
    return rest - last.astype(f32)


def solution(mesh):
    layers, cols = mesh.shape["layer"], mesh.shape["col"]
    ring = (layers, cols) == (8, 4)
    return jax.shard_map(
        local_ring if ring else local_plain,
        mesh=mesh,
        in_specs=(
            P("layer", None, "col"),
            P("layer", None, "col"),
            P("layer", None, None),
            P("layer", None, None),
            P(),
            P("layer", "col"),
        ),
        out_specs=P("layer", "col"),
        check_vma=False,
    )
```
